32 devices in a mesh: groups: 2 (over x), tm: 16 (over z, y, core).
Axes of the slice: x: 2, y: 2, z: 4, core: 2. Of those that a mesh axis runs over, the one named last changes fastest.
Arguments:
- initial_value: float32 [1024, 1024], P('groups'), parts along dimension 0, may hold values from -3 to 3
- guess: float32 [32, 512, 1024], P(('groups', 'tm')), parts along dimension 0, may hold values from -3 to 3
- rate_field: float32 [512, 1024], replicated, may hold values from 0.1 to 1
- strength: float32 [2], P('groups'), parts along dimension 0, may hold values from 0.2 to 0.8
Outputs:
- solution: float32 [32, 512, 1024], P(('groups', 'tm')), parts along dimension 0
The draws below stay inside these ranges and needn't reach their ends.
There are 2 independent parts, one for each index of `groups`. The reference program is written for one: setup_inputs(seed, part) draws one part's arguments, and reference() takes and returns one part's arrays. A program takes and returns all parts, laid end to end along the dimension named above; an argument that names none is the same for every part. Nothing has to cross between parts.
All inputs are finite; a program needn't handle non-finite values.
Results may differ from the reference program's by a relative error of at most 0.0003.
Values sent between devices are 32-bit elements; how exact they have to be, the bound alone decides.
No kernel may reach another device: no remote copies, remote signals or barrier semaphores. Data moves between devices by JAX's collectives and lax.ppermute only.
A program may use at most 64 MiB of HBM per device.

```python
import math
import jax
import jax.numpy as jnp
from jax import lax

NX = 512
NY = 1024
SWEEPS = 2
STEPS = 16


def shard_levels(key, dims, pieces, smallest, high):
    def one(position, blocks):
        draws = jax.random.uniform(jax.random.fold_in(jax.random.fold_in(key, 6), position), (blocks,), jnp.float32, smallest / len(pieces), high / len(pieces))
        return jnp.repeat(jnp.exp(draws), dims[position] // blocks).reshape((-1,) + (1,) * (len(dims) - position - 1))

    level = one(*pieces[0])
    for cut in pieces[1:]:
        level = level * one(*cut)
    return level


def scatter_about(own_key, shape, deviation, bound, cuts=(), kind=jnp.bfloat16):
    array = jax.random.normal(own_key, shape, jnp.float32) * deviation
    if len(cuts) > 0:
        array = shard_levels(own_key, shape, cuts, -0.22, 0.18) * array
    return jnp.clip(array, min=-bound, max=bound).astype(kind)


def setup_inputs(seed: int = 0, part: int = 0) -> dict:
    key_of = jax.random.split(jax.random.key(seed), 5)
    part_keys = jax.random.split(jax.random.fold_in(key_of[4], part), 5)
    return {
        "initial_value": scatter_about(part_keys[0], (NX, NY), 0.5, 3.0, (), jnp.float32),
        "guess": scatter_about(part_keys[1], (STEPS, NX, NY), 0.5, 3.0, ((0, 16),), jnp.float32),
        "rate_field": jnp.clip(jnp.exp(jax.random.uniform(key_of[2], (NX, NY), jnp.float32, math.log(0.1), math.log(1.0))), 0.1, 1.0),
        "strength": jnp.clip(jnp.exp(jax.random.uniform(part_keys[3], (1,), jnp.float32, math.log(0.2), math.log(0.8))), 0.2, 0.8),
    }


alpha_factor = 0.05
diffusion = 1.0
linear_part = 0.5
highest = lax.Precision.HIGHEST

def sine_table(order_n):
    ramp = jnp.arange(order_n, dtype=jnp.int32) + 1
    folded = ramp[:, None] * ramp[None, :] % (2 * (order_n + 1))
    return math.sqrt(2.0 / (order_n + 1)) * jnp.sin(jnp.pi * folded.astype(jnp.float32) / (order_n + 1))

def sine_eigen(ramp_rows, order_n):
    angle = jnp.pi * (ramp_rows.astype(jnp.float32) + 1.0) / (2.0 * (order_n + 1))
    sines = jnp.sin(angle)
    return 4.0 * sines * sines

def time_tables(step_count):
    ramp = jnp.arange(step_count, dtype=jnp.int32)
    folded = ramp[:, None] * ramp[None, :] % step_count
    angle = 2.0 * jnp.pi * folded.astype(jnp.float32) / step_count
    return (jnp.cos(angle), jnp.sin(angle))

def laplace(surface):
    padded = jnp.pad(surface, 1)
    return padded[2:, 1:-1] + padded[:-2, 1:-1] + padded[1:-1, 2:] + padded[1:-1, :-2] - 4.0 * surface

def operator(surface, rate_field, strength_value):
    return surface - diffusion * laplace(surface) + strength_value * rate_field * surface * (1.0 + surface * surface)

def to_sine(surface, row_table, col_table):
    return jnp.dot(jnp.dot(row_table, surface, precision=highest), col_table, precision=highest)

def modal_solve(flat, cos_t, sin_t, real_den, imag_den, step_count):
    part_re = jnp.dot(cos_t, flat, precision=highest)
    part_im = -jnp.dot(sin_t, flat, precision=highest)
    magnitude = real_den * real_den + imag_den * imag_den
    sol_re = -(part_re * real_den + part_im * imag_den) / magnitude
    sol_im = -(part_im * real_den - part_re * imag_den) / magnitude
    return (jnp.dot(cos_t, sol_re, precision=highest) - jnp.dot(sin_t, sol_im, precision=highest)) / step_count

def reference(initial_value, guess, rate_field, strength):
    step_count = guess.shape[0]
    row_table = sine_table(NX)
    col_table = sine_table(NY)
    strength_value = strength[0]
    log_ratio = math.log(alpha_factor) / step_count
    ratio_g = math.exp(log_ratio)
    scaling = jnp.exp(jnp.arange(step_count, dtype=jnp.int32).astype(jnp.float32) * log_ratio)
    cos_t, sin_t = time_tables(step_count)
    eigen_sum = (sine_eigen(jnp.arange(NX, dtype=jnp.int32), NX)[:, None] + sine_eigen(jnp.arange(NY, dtype=jnp.int32), NY)[None, :]).reshape(-1)
    real_den = (1.0 + linear_part * strength_value - ratio_g * cos_t[:, 1])[:, None] + diffusion * eigen_sum[None, :]
    imag_den = (ratio_g * sin_t[:, 1])[:, None]

    def residual_step(couple):
        return to_sine(operator(couple[0], rate_field, strength_value) - couple[1], row_table, col_table)

    def back_step(surface):
        return to_sine(surface, row_table, col_table)
    state = guess
    for sweep_index in range(SWEEPS):
        earlier = jnp.concatenate([initial_value[None], state[:-1]], axis=0)
        spectral = lax.map(residual_step, (state, earlier))
        scaled = (spectral * scaling[:, None, None]).reshape(step_count, -1)
        solved = modal_solve(scaled, cos_t, sin_t, real_den, imag_den, step_count).reshape(state.shape)
        solved = solved / scaling[:, None, None]
        state = state + lax.map(back_step, solved)
    return state
```

```python
import math

import jax
import jax.numpy as jnp
import numpy as np
from jax import lax
from jax.experimental import pallas as pl
from jax.experimental.pallas import tpu as pltpu
from jax.sharding import PartitionSpec as P

SWEEPS = 2

alpha_factor = 0.05
diffusion = 1.0
linear_part = 0.5
f32 = jnp.float32
bf16 = jnp.bfloat16
VMEM = pl.BlockSpec(memory_space=pltpu.VMEM)
SMEM = pl.BlockSpec(memory_space=pltpu.SMEM)


def halves(matrix):
    high = matrix.astype(bf16)
    low = (matrix - high.astype(np.float64)).astype(bf16)
    return high, low


def sine_halves(order):
    ramp = np.arange(order, dtype=np.int64) + 1
    folded = ramp[:, None] * ramp[None, :] % (2 * (order + 1))
    full = math.sqrt(2.0 / (order + 1)) * np.sin(np.pi * folded / (order + 1))
    half = order // 2
    return np.stack([full[0::2, :half], full[1::2, :half]])


def sine_eigen(order):
    ramp = np.arange(order, dtype=np.float64)
    value = 4.0 * np.sin(np.pi * (ramp + 1.0) / (2.0 * (order + 1))) ** 2
    return np.concatenate([value[0::2], value[1::2]]).astype(np.float32)


def reversal(size):
    return np.eye(size)[::-1].astype(bf16)


def split(value):
    high = value.astype(bf16)
    return high, (value - high.astype(f32)).astype(bf16)


def product(left, right, dims):
    return lax.dot_general(left, right, ((dims), ((), ())), preferred_element_type=f32)


def apply_right(value, high, low, transposed):
    dims = ((1,), (0,)) if transposed else ((1,), (1,))
    top, rest = split(value)
    return product(top, high, dims) + (product(top, low, dims) + product(rest, high, dims))


def apply_left(high, low, value):
    dims = ((1,), (0,))
    top, rest = split(value)
    return product(high, top, dims) + (product(low, top, dims) + product(high, rest, dims))


def flip_rows(value, mirror):
    size = mirror.shape[0]
    count = value.shape[0] // size
    pieces = []
    for index in range(count):
        block = value[(count - 1 - index) * size : (count - index) * size]
        top, rest = split(block)
        dims = ((1,), (0,))
        pieces.append(product(mirror, top, dims) + product(mirror, rest, dims))
    return pieces[0] if count == 1 else jnp.concatenate(pieces, axis=0)


def flip_cols(value, mirror):
    size = mirror.shape[0]
    count = value.shape[1] // size
    pieces = []
    for index in range(count):
        block = value[:, (count - 1 - index) * size : (count - index) * size]
        top, rest = split(block)
        dims = ((1,), (0,))
        pieces.append(product(top, mirror, dims) + product(rest, mirror, dims))
    return pieces[0] if count == 1 else jnp.concatenate(pieces, axis=1)


def react(state, rate, strength):
    return strength * state * (linear_part - rate * (1.0 + state * state))


def to_modes(get, tables, write):
    sxh, sxl, syh, syl = tables
    for col in range(2):
        for row in range(2):
            sign_r = 1.0 if row == 0 else -1.0
            sign_c = 1.0 if col == 0 else -1.0
            left = get(0, 0) + sign_r * get(1, 0)
            right = get(0, 1) + sign_r * get(1, 1)
            part = left + sign_c * right
            part = apply_right(part, syh[col], syl[col], False)
            write(row, col, apply_left(sxh[row], sxl[row], part))


def from_modes(get, tables):
    txh, txl, syh, syl = tables
    part = [[None, None], [None, None]]
    for col in range(2):
        for row in range(2):
            back = apply_left(txh[row], txl[row], get(row, col))
            part[row][col] = apply_right(back, syh[col], syl[col], True)
    rows = []
    for row in range(2):
        even, odd = part[row]
        rows.append((even + odd, even - odd))
    return [
        [rows[0][half] + rows[1][half] for half in range(2)],
        [rows[0][half] - rows[1][half] for half in range(2)],
    ]


def gain(shift, mu_row, mu_col):
    return 1.0 / (shift + diffusion * (mu_row + mu_col))


def first_kernel(strength, place, u, rate, first, mur, muc, sxh, sxl, syh, syl, mirx, miry, even, odd, even_up, odd_up, fold):
    rows, cols = u.shape
    hr, hc = rows // 2, cols // 2
    s = strength[0]
    shift = 1.0 + linear_part * s
    outs, ups = (even, odd), (even_up, odd_up)

    def folded(value):
        bottom = flip_rows(value[hr:], mirx[...])
        top = value[:hr]
        return top[:, :hc], flip_cols(top[:, hc:], miry[...]), bottom[:, :hc], flip_cols(bottom[:, hc:], miry[...])

    def fill(value):
        a, b, c, d = folded(value)
        fold[:hr, :hc], fold[:hr, hc:], fold[hr:, :hc], fold[hr:, hc:] = a, b, c, d

    def get(row, col):
        return fold[row * hr : (row + 1) * hr, col * hc : (col + 1) * hc]

    tables = (sxh, sxl, syh, syl)
    fill(react(u[...], rate[...], s) + jnp.where(place[0] == 0, 1.0, 0.0) * first[...])

    def write(row, col, modes):
        block = slice(row * hr, (row + 1) * hr)
        value = modes * gain(shift, mur[block, :], muc[:, col * hc : (col + 1) * hc])
        outs[col][block, :] = value
        ups[col][block, :] = value

    to_modes(get, tables, write)

    @pl.when(place[0] == place[1] - 1)
    def _():
        fill(u[...])

        def lower(row, col, modes):
            block = slice(row * hr, (row + 1) * hr)
            ups[col][block, :] = ups[col][block, :] - modes

        to_modes(get, tables, lower)


def middle_kernel(strength, place, ve, vo, rate, first, mur, muc, sxh, sxl, txh, txl, syh, syl, even, odd, even_up, odd_up, fold):
    hr, hc = ve.shape[0] // 2, ve.shape[1]
    s = strength[0]
    shift = 1.0 + linear_part * s
    modes_in, outs, ups = (ve, vo), (even, odd), (even_up, odd_up)
    quads = from_modes(lambda r, c: modes_in[c][r * hr : (r + 1) * hr, :], (txh, txl, syh, syl))
    for r in range(2):
        for c in range(2):
            spot = (slice(r * hr, (r + 1) * hr), slice(c * hc, (c + 1) * hc))
            fold[spot] = react(quads[r][c], rate[spot], s) + first[spot]

    def get(row, col):
        return fold[row * hr : (row + 1) * hr, col * hc : (col + 1) * hc]

    last = jnp.where(place[0] == place[1] - 1, 1.0, 0.0)

    def write(row, col, modes):
        block = slice(row * hr, (row + 1) * hr)
        value = modes * gain(shift, mur[block, :], muc[:, col * hc : (col + 1) * hc])
        outs[col][block, :] = value
        ups[col][block, :] = value - last * modes_in[col][block, :]

    to_modes(get, (sxh, sxl, syh, syl), write)


def last_kernel(ve, vo, txh, txl, syh, syl, mirx, miry, out):
    hr, hc = ve.shape[0] // 2, ve.shape[1]
    modes_in = (ve, vo)
    quads = from_modes(lambda r, c: modes_in[c][r * hr : (r + 1) * hr, :], (txh, txl, syh, syl))
    out[:hr, :hc] = quads[0][0]
    out[:hr, hc:] = flip_cols(quads[0][1], miry[...])
    out[hr:, :hc] = flip_rows(quads[1][0], mirx[...])
    out[hr:, hc:] = flip_rows(flip_cols(quads[1][1], miry[...]), mirx[...])


def fold_kernel(place, rate, first, mirx, miry, rate_out, first_out):
    hr, hc = rate.shape[0] // 2, rate.shape[1] // 2
    start = jnp.where(place[0] == 0, 1.0, 0.0)
    for value, out, scale in ((rate, rate_out, 1.0), (first, first_out, start)):
        out[:hr, :hc] = scale * value[:hr, :hc]
        out[:hr, hc:] = scale * flip_cols(value[:hr, hc:], miry[...])
        bottom = scale * flip_rows(value[hr:], mirx[...])
        out[hr:, :hc] = bottom[:, :hc]
        out[hr:, hc:] = flip_cols(bottom[:, hc:], miry[...])


def params():
    return pltpu.CompilerParams(vmem_limit_bytes=48 << 20)


def scan_steps(field, up, count, position, gains):
    levels = count.bit_length() - 1
    total = up
    row = jnp.int32(0)
    kept = []
    for level in range(levels):
        step = 1 << level
        pairs = [(source, source ^ step) for source in range(count)]
        half = total.shape[0] // 2
        bit = (position >> level) & 1
        send = lax.dynamic_slice_in_dim(total, (1 - bit) * half, half)
        keep = lax.dynamic_slice_in_dim(total, bit * half, half)
        got = lax.ppermute(send, "tm", pairs)
        row = row + bit * half
        low = jnp.where(bit == 0, keep, got)
        high = jnp.where(bit == 0, got, keep)
        factor = gains(row, half, step)
        total = high + factor * low
        kept.append((low, factor, bit, pairs))
    full_gain = gains(row, total.shape[0], count)
    carry = alpha_factor * total / (1.0 - alpha_factor * full_gain)
    for low, factor, bit, pairs in reversed(kept):
        later = low + factor * carry
        own = jnp.where(bit == 0, carry, later)
        send = jnp.where(bit == 0, later, carry)
        got = lax.ppermute(send, "tm", pairs)
        carry = jnp.concatenate([jnp.where(bit == 0, own, got), jnp.where(bit == 0, got, own)], axis=0)
    return field + gains(jnp.int32(0), field.shape[0], 1) * carry


def body(initial_value, guess, rate_field, strength):
    count = lax.axis_size("tm")
    position = lax.axis_index("tm")
    state = guess[0]
    rows, cols = state.shape
    hr, hc = rows // 2, cols // 2
    shift = 1.0 + linear_part * strength[0]
    place = jnp.stack([position, jnp.int32(count)])

    tx, ty = sine_halves(rows), sine_halves(cols)
    sxh, sxl = (jnp.asarray(t) for t in halves(tx))
    txh, txl = (jnp.asarray(t) for t in halves(tx.transpose(0, 2, 1)))
    syh, syl = (jnp.asarray(t) for t in halves(ty))
    mirx = jnp.asarray(reversal(math.gcd(hr, 256)))
    miry = jnp.asarray(reversal(math.gcd(hc, 256)))
    mu_row, mu_col = jnp.asarray(sine_eigen(rows)), jnp.asarray(sine_eigen(cols))
    mur, muc = mu_row[:, None], mu_col[None, :]

    chunk = jax.ShapeDtypeStruct((rows, hc), f32)
    scratch = [pltpu.VMEM((rows, cols), f32)]

    def gains_of(col):
        def gains(row, height, power):
            piece = lax.dynamic_slice_in_dim(mu_row, row, height)
            value = gain(shift, piece[:, None], mu_col[None, col * hc : (col + 1) * hc])
            while power > 1:
                value = value * value
                power //= 2
            return value

        return gains

    field_up = pl.pallas_call(
        first_kernel,
        out_shape=[chunk] * 4,
        in_specs=[SMEM] * 2 + [VMEM] * 11,
        out_specs=[VMEM] * 4,
        scratch_shapes=scratch,
        compiler_params=params(),
        name="first",
    )(strength, place, state, rate_field, initial_value, mur, muc, sxh, sxl, syh, syl, mirx, miry)
    rate_folded, first_folded = pl.pallas_call(
        fold_kernel,
        out_shape=[jax.ShapeDtypeStruct((rows, cols), f32)] * 2,
        in_specs=[SMEM] + [VMEM] * 4,
        out_specs=[VMEM] * 2,
        compiler_params=params(),
        name="fold",
    )(place, rate_field, initial_value, mirx, miry)
    for sweep_index in range(SWEEPS):
        modes = []
        for col in range(2):
            with jax.named_scope(f"scan_{sweep_index}_{col}"):
                modes.append(scan_steps(field_up[col], field_up[2 + col], count, position, gains_of(col)))
        if sweep_index < SWEEPS - 1:
            field_up = pl.pallas_call(
                middle_kernel,
                out_shape=[chunk] * 4,
                in_specs=[SMEM] * 2 + [VMEM] * 12,
                out_specs=[VMEM] * 4,
                scratch_shapes=scratch,
                compiler_params=params(),
                name="middle",
            )(strength, place, *modes, rate_folded, first_folded, mur, muc, sxh, sxl, txh, txl, syh, syl)
    result = pl.pallas_call(
        last_kernel,
        out_shape=jax.ShapeDtypeStruct((rows, cols), f32),
        in_specs=[VMEM] * 8,
        out_specs=VMEM,
        compiler_params=params(),
        name="last",
    )(*modes, txh, txl, syh, syl, mirx, miry)
    return result[None]


def solution(mesh):
    in_specs = (P("groups", None), P(("groups", "tm"), None, None), P(), P("groups"))
    out_specs = P(("groups", "tm"), None, None)
    return jax.shard_map(body, mesh=mesh, in_specs=in_specs, out_specs=out_specs, check_vma=False)
```

```python
import math

import jax
import jax.numpy as jnp
import numpy as np
from jax import lax
from jax.experimental import pallas as pl
from jax.experimental.pallas import tpu as pltpu
from jax.sharding import PartitionSpec as P

SWEEPS = 2

alpha_factor = 0.05
diffusion = 1.0
linear_part = 0.5
f32 = jnp.float32
bf16 = jnp.bfloat16
VMEM = pl.BlockSpec(memory_space=pltpu.VMEM)
SMEM = pl.BlockSpec(memory_space=pltpu.SMEM)
ANY = pl.BlockSpec(memory_space=pl.ANY)
HBM = pl.BlockSpec(memory_space=pltpu.HBM)


def halves(matrix):
    high = matrix.astype(bf16)
    low = (matrix - high.astype(np.float64)).astype(bf16)
    return high, low


def sine_halves(order):
    ramp = np.arange(order, dtype=np.int64) + 1
    folded = ramp[:, None] * ramp[None, :] % (2 * (order + 1))
    full = math.sqrt(2.0 / (order + 1)) * np.sin(np.pi * folded / (order + 1))
    half = order // 2
    return np.stack([full[0::2, :half], full[1::2, :half]])


def sine_eigen(order):
    ramp = np.arange(order, dtype=np.float64)
    value = 4.0 * np.sin(np.pi * (ramp + 1.0) / (2.0 * (order + 1))) ** 2
    return np.concatenate([value[0::2], value[1::2]]).astype(np.float32)


def reversal(size):
    return np.eye(size)[::-1].astype(bf16)


def split(value):
    high = value.astype(bf16)
    return high, (value - high.astype(f32)).astype(bf16)


def product(left, right, dims=((1,), (0,))):
    return lax.dot_general(left, right, (dims, ((), ())), preferred_element_type=f32)


def apply_right(value, high, low, dims):
    top, rest = split(value)
    return product(top, high, dims) + (product(top, low, dims) + product(rest, high, dims))


def apply_left(high, low, value):
    top, rest = split(value)
    return product(high, top) + (product(low, top) + product(high, rest))


def forward(value, sx, sy):
    return apply_left(*sx, apply_right(value, *sy, ((1,), (1,))))


def backward(modes, tx, sy):
    return apply_right(apply_left(*tx, modes), *sy, ((1,), (0,)))


def flip_rows(value, mirror):
    size = mirror.shape[0]
    count = value.shape[0] // size
    pieces = []
    for index in range(count):
        top, rest = split(value[(count - 1 - index) * size : (count - index) * size])
        pieces.append(product(mirror, top) + product(mirror, rest))
    return pieces[0] if count == 1 else jnp.concatenate(pieces, axis=0)


def flip_cols(value, mirror):
    size = mirror.shape[0]
    count = value.shape[1] // size
    pieces = []
    for index in range(count):
        top, rest = split(value[:, (count - 1 - index) * size : (count - index) * size])
        pieces.append(product(top, mirror) + product(rest, mirror))
    return pieces[0] if count == 1 else jnp.concatenate(pieces, axis=1)


def react(state, rate, strength):
    return strength * state * (linear_part - rate * (1.0 + state * state))


def gain(base_row, base_col, power=1):
    value = 1.0 / (base_row + base_col)
    while power > 1:
        value = value * value
        power //= 2
    return value


def bit_of(place, level):
    return lax.shift_right_logical(place[0], jnp.int32(level)) & 1


def kept_row(place, rows, level):
    row = jnp.int32(0)
    for index in range(level + 1):
        row = row + bit_of(place, index) * (rows >> (index + 1))
    return pl.multiple_of(row, math.gcd(rows >> (level + 1), 8))


def is_last(place):
    return place[0] == place[1] - 1


def butterfly(quads, sign_r):
    left = quads[0][0] + sign_r * quads[1][0]
    right = quads[0][1] + sign_r * quads[1][1]
    return left + right, left - right


def write_modes(place, modes, row, base_row, base_col, field, send, keep, less):
    hr = send.shape[0]
    block = pl.ds(pl.multiple_of(row * hr, 8), hr)
    value = modes * gain(base_row[block, :], base_col[...])
    field[block, :] = value
    upward = value if less is None else value - less
    bit = bit_of(place, 0)

    @pl.when(bit == row)
    def _():
        keep[...] = upward

    @pl.when(bit != row)
    def _():
        send[...] = upward


def first_kernel(strength, place, u_hbm, rate_hbm, first_hbm, sxh_hbm, sxl_hbm, syh_hbm, syl_hbm, mirx_hbm, miry_hbm, base_row, base_col, field, send, keep, x_odd, xu_odd, u, rate, first, sxh, sxl, syh, syl, mirx, miry, x_even, sems):
    rows, cols = u.shape
    hr, hc = rows // 2, cols // 2
    s = strength[0]
    sources = (u_hbm, rate_hbm, mirx_hbm, miry_hbm, syh_hbm.at[0], syl_hbm.at[0], sxh_hbm, sxl_hbm)
    targets = (u, rate, mirx, miry, syh, syl, sxh, sxl)
    copies = [pltpu.make_async_copy(a, b, sems.at[i]) for i, (a, b) in enumerate(zip(sources, targets))]
    start = pltpu.make_async_copy(first_hbm, first, sems.at[len(copies)])
    for copy in copies:
        copy.start()

    @pl.when(place[0] == 0)
    def _():
        start.start()

    for copy in copies[:4]:
        copy.wait()

    def fold(value, even, odd):
        bottom = flip_rows(value[hr:], mirx[...])
        top = value[:hr]
        quads = (
            (top[:, :hc], flip_cols(top[:, hc:], miry[...])),
            (bottom[:, :hc], flip_cols(bottom[:, hc:], miry[...])),
        )
        for row, sign in enumerate((1.0, -1.0)):
            even[row], odd[row] = butterfly(quads, sign)

    rate[...] = react(u[...], rate[...], s)

    @pl.when(place[0] == 0)
    def _():
        start.wait()
        rate[...] = rate[...] + first[...]

    fold(rate[...], x_even, x_odd)
    for copy in copies[4:]:
        copy.wait()

    @pl.loop(0, 2)
    def _(row):
        modes = forward(x_even[row], (sxh[row], sxl[row]), (syh[...], syl[...]))
        write_modes(place, modes, row, base_row, base_col, field, send, keep, None)

    @pl.when(is_last(place))
    def _():
        fold(u[...], x_even, xu_odd)

        @pl.loop(0, 2)
        def _(row):
            modes = forward(x_even[row], (sxh[row], sxl[row]), (syh[...], syl[...]))

            @pl.when(bit_of(place, 0) == row)
            def _():
                keep[...] = keep[...] - modes

            @pl.when(bit_of(place, 0) != row)
            def _():
                send[...] = send[...] - modes


def second_kernel(place, x_odd, xu_odd, sxh, sxl, syh, syl, base_row, base_col, order, field, send, keep):
    @pl.loop(0, 2)
    def _(row):
        modes = forward(x_odd[row], (sxh[row], sxl[row]), (syh[1], syl[1]))
        write_modes(place, modes, row, base_row, base_col, field, send, keep, None)

    @pl.when(is_last(place))
    def _():
        @pl.loop(0, 2)
        def _(row):
            modes = forward(xu_odd[row], (sxh[row], sxl[row]), (syh[1], syl[1]))

            @pl.when(bit_of(place, 0) == row)
            def _():
                keep[...] = keep[...] - modes

            @pl.when(bit_of(place, 0) != row)
            def _():
                send[...] = send[...] - modes


def later_second_kernel(place, x_odd, v_odd, sxh, sxl, syh, syl, base_row, base_col, order, field, send, keep):
    hr = send.shape[0]
    last = jnp.where(is_last(place), 1.0, 0.0)

    @pl.loop(0, 2)
    def _(row):
        modes = forward(x_odd[row], (sxh[row], sxl[row]), (syh[1], syl[1]))
        less = last * v_odd[pl.ds(pl.multiple_of(row * hr, 8), hr), :]
        write_modes(place, modes, row, base_row, base_col, field, send, keep, less)


def fold_kernel(place, rate, first, mirx, miry, order, rate_out, first_out):
    hr, hc = rate.shape[0] // 2, rate.shape[1] // 2

    def fold(value, out):
        out[:hr, :hc] = value[:hr, :hc]
        out[:hr, hc:] = flip_cols(value[:hr, hc:], miry[...])
        bottom = flip_rows(value[hr:], mirx[...])
        out[hr:, :hc] = bottom[:, :hc]
        out[hr:, hc:] = flip_cols(bottom[:, hc:], miry[...])

    fold(rate, rate_out)

    @pl.when(place[0] == 0)
    def _():
        fold(first, first_out)

    @pl.when(place[0] != 0)
    def _():
        first_out[...] = jnp.zeros_like(first_out)


def rise_kernel(level, rows, place, keep, got, base_row, base_col, order, *outs):
    low = outs[0]
    half = keep.shape[0]
    bit = bit_of(place, level)
    row = kept_row(place, rows, level)
    own, other = keep[...], got[...]
    low[...] = jnp.where(bit == 0, own, other)
    factor = gain(base_row[pl.ds(row, half), :], base_col[...], 1 << level)
    total = jnp.where(bit == 0, other, own) + factor * low[...]
    if len(outs) == 2:
        outs[1][...] = total
        return
    quarter = half // 2
    send, keep_out = outs[1:]
    upper = bit_of(place, level + 1)
    send[...] = jnp.where(upper == 0, total[quarter:], total[:quarter])
    keep_out[...] = jnp.where(upper == 0, total[:quarter], total[quarter:])


def descend(place, level, rows, low, carry, base_row, base_col, own, send):
    half = low.shape[0]
    factor = gain(base_row[pl.ds(kept_row(place, rows, level), half), :], base_col[...], 1 << level)
    later = low[...] + factor * carry
    bit = bit_of(place, level)
    own[...] = jnp.where(bit == 0, carry, later)
    send[...] = jnp.where(bit == 0, later, carry)


def top_kernel(level, rows, place, mine, got, low, base_row, base_col, order, own, send):
    height = mine.shape[0]
    bit = bit_of(place, level)
    spot = pl.ds(kept_row(place, rows, level - 1), height)
    value = 1.0 / (base_row[spot, :] + base_col[...])
    factor = value
    for _ in range(level):
        factor = factor * factor
    early = jnp.where(bit == 0, mine[...], got[...])
    late = jnp.where(bit == 0, got[...], mine[...])
    carry = alpha_factor * (late + factor * early) / (1.0 - alpha_factor * (factor * factor))
    carry = jnp.where(bit == 0, carry, early + factor * carry)
    descend(place, level - 1, rows, low, carry, base_row, base_col, own, send)


def fall_kernel(level, rows, place, own_in, got, low, base_row, base_col, order, own, send):
    bit = bit_of(place, level + 1)
    first = jnp.where(bit == 0, own_in[...], got[...])
    second = jnp.where(bit == 0, got[...], own_in[...])
    carry = jnp.concatenate([first, second], axis=0)
    descend(place, level, rows, low, carry, base_row, base_col, own, send)


def new_modes(place, row, field, own, got, base_row, base_col):
    hr = own.shape[0]
    block = pl.ds(pl.multiple_of(row * hr, 8), hr)
    carry = jnp.where(bit_of(place, 0) == row, own[...], got[...])
    return field[block, :] + gain(base_row[block, :], base_col[...]) * carry


def half_back_kernel(place, field, own, got, base_row, base_col, txh, txl, syh, syl, order, cells, *v_out):
    hr = own.shape[0]
    for row in range(2):
        modes = new_modes(place, row, field, own, got, base_row, base_col)
        if v_out:
            v_out[0][row * hr : (row + 1) * hr, :] = modes
        part = backward(modes, (txh[row], txl[row]), (syh[0], syl[0]))
        if row == 0:
            cells[:hr, :], cells[hr:, :] = part, part
        else:
            cells[:hr, :] = cells[:hr, :] + part
            cells[hr:, :] = cells[hr:, :] - part


def odd_cells(place, field, own, got, base_row, base_col, txh, txl, syh, syl, v_out):
    hr = own.shape[0]
    parts = []
    for row in range(2):
        modes = new_modes(place, row, field, own, got, base_row, base_col)
        if v_out is not None:
            v_out[row * hr : (row + 1) * hr, :] = modes
        parts.append(backward(modes, (txh[row], txl[row]), (syh[1], syl[1])))
    return parts[0] + parts[1], parts[0] - parts[1]


def middle_kernel(strength, place, field_in, own, got, cells, v_even, rate, first, base_row, base_even, base_odd, sxh, sxl, txh, txl, syh, syl, field, send, keep, x_odd, v_odd, x_even):
    hr, hc = own.shape
    s = strength[0]
    odd = odd_cells(place, field_in, own, got, base_row, base_odd, txh, txl, syh, syl, v_odd)
    quads = []
    for half in range(2):
        rows = slice(half * hr, (half + 1) * hr)
        even = cells[rows, :]
        quads.append(
            (
                react(even + odd[half], rate[rows, :hc], s) + first[rows, :hc],
                react(even - odd[half], rate[rows, hc:], s) + first[rows, hc:],
            )
        )
    for row, sign in enumerate((1.0, -1.0)):
        x_even[row], x_odd[row] = butterfly(quads, sign)
    last = jnp.where(is_last(place), 1.0, 0.0)

    @pl.loop(0, 2)
    def _(row):
        modes = forward(x_even[row], (sxh[row], sxl[row]), (syh[0], syl[0]))
        less = last * v_even[pl.ds(pl.multiple_of(row * hr, 8), hr), :]
        write_modes(place, modes, row, base_row, base_even, field, send, keep, less)


def last_kernel(place, field_in, own, got, cells, base_row, base_odd, txh, txl, syh, syl, mirx, miry, out):
    hr, hc = own.shape
    odd = odd_cells(place, field_in, own, got, base_row, base_odd, txh, txl, syh, syl, None)
    out[:hr, :hc] = cells[:hr, :] + odd[0]
    out[:hr, hc:] = flip_cols(cells[:hr, :] - odd[0], miry[...])
    bottom = flip_rows(jnp.concatenate([cells[hr:, :] + odd[1], cells[hr:, :] - odd[1]], axis=1), mirx[...])
    out[hr:, :hc] = bottom[:, :hc]
    out[hr:, hc:] = flip_cols(bottom[:, hc:], miry[...])


def run(kernel, name, outs, operands, specs, limit, scratch=()):
    return pl.pallas_call(
        kernel,
        out_shape=[jax.ShapeDtypeStruct(shape, f32) for shape in outs],
        in_specs=specs,
        out_specs=[VMEM] * len(outs),
        scratch_shapes=list(scratch),
        compiler_params=pltpu.CompilerParams(vmem_limit_bytes=limit << 20),
        cost_estimate=pl.CostEstimate(flops=0, bytes_accessed=1024, transcendentals=0),
        name=name,
    )(*operands)


def body(initial_value, guess, rate_field, strength):
    count = lax.axis_size("tm")
    levels = count.bit_length() - 1
    position = lax.axis_index("tm")
    state = guess[0]
    rows, cols = state.shape
    hr, hc = rows // 2, cols // 2
    half_shift = 0.5 * (1.0 + linear_part * strength[0])
    place = jnp.stack([position, jnp.int32(count)])

    tx, ty = sine_halves(rows), sine_halves(cols)
    sx = tuple(jnp.asarray(t) for t in halves(tx))
    back_x = tuple(jnp.asarray(t) for t in halves(tx.transpose(0, 2, 1)))
    sy = tuple(jnp.asarray(t) for t in halves(ty))
    mirx = jnp.asarray(reversal(math.gcd(hr, 256)))
    miry = jnp.asarray(reversal(math.gcd(hc, 256)))
    base_row = half_shift + diffusion * jnp.asarray(sine_eigen(rows))[:, None]
    base_cols = half_shift + diffusion * jnp.asarray(sine_eigen(cols))[None, :]
    base_col = (base_cols[:, :hc], base_cols[:, hc:])

    def travel(value, level):
        return lax.ppermute(value, "tm", [(source, source ^ (1 << level)) for source in range(count)])

    chunk, half = (rows, hc), (hr, hc)
    pair = (2, hr, hc)
    field = [None, None]
    keep = [None, None]
    flying = [None, None]

    field[0], send, keep[0], x_odd, extra = run(
        first_kernel,
        "first",
        [chunk, half, half, pair, pair],
        (strength, place, state, rate_field, initial_value, *sx, *sy, mirx, miry, base_row, base_col[0]),
        [SMEM] * 2 + [HBM] * 9 + [VMEM] * 2,
        40,
        [pltpu.VMEM((rows, cols), f32)] * 3
        + [pltpu.VMEM((2, hr, hr), bf16)] * 2
        + [pltpu.VMEM((hc, hc), bf16)] * 2
        + [pltpu.VMEM(mirx.shape, bf16), pltpu.VMEM(miry.shape, bf16), pltpu.VMEM(pair, f32)]
        + [pltpu.SemaphoreType.DMA((9,))],
    )
    flying[0] = travel(send, 0)
    order = send
    second = second_kernel
    rate_folded = first_folded = None

    for sweep in range(SWEEPS):
        final = sweep == SWEEPS - 1
        field[1], send, keep[1] = run(
            second,
            f"second_{sweep}",
            [chunk, half, half],
            (place, x_odd, extra, *sx, *sy, base_row, base_col[1], order),
            [SMEM] + [VMEM] * 8 + [ANY],
            20,
        )
        flying[1] = travel(send, 0)
        order = send
        low = [[], []]
        own = [None, None]
        for level in range(levels - 1):
            for col in range(2):
                height = rows >> (level + 1)
                full = level == levels - 2
                shapes = [(height, hc)] + ([(height, hc)] if full else [(height // 2, hc)] * 2)
                outs = run(
                    lambda *refs, level=level: rise_kernel(level, rows, *refs),
                    f"rise_{sweep}_{level}_{col}",
                    shapes,
                    (place, keep[col], flying[col], base_row, base_col[col], order),
                    [SMEM] + [VMEM] * 4 + [ANY],
                    8,
                )
                low[col].append(outs[0])
                keep[col] = outs[-1]
                order = outs[1]
                flying[col] = travel(outs[1], level + 1)
            if sweep == 0 and level == 0:
                rate_folded, first_folded = run(
                    fold_kernel,
                    "fold",
                    [(rows, cols)] * 2,
                    (place, rate_field, initial_value, mirx, miry, order),
                    [SMEM] + [VMEM] * 4 + [ANY],
                    24,
                )
                order = rate_folded
        for level in range(levels - 2, -1, -1):
            for col in range(2):
                height = rows >> (level + 1)
                top = level == levels - 2
                kernel = (
                    (lambda *refs: top_kernel(levels - 1, rows, *refs))
                    if top
                    else (lambda *refs, level=level: fall_kernel(level, rows, *refs))
                )
                own[col], send = run(
                    kernel,
                    f"fall_{sweep}_{level}_{col}",
                    [(height, hc)] * 2,
                    (place, keep[col] if top else own[col], flying[col], low[col][level], base_row, base_col[col], order),
                    [SMEM] + [VMEM] * 5 + [ANY],
                    8,
                )
                order = send
                flying[col] = travel(send, level)
        outs = run(
            half_back_kernel,
            f"back_{sweep}",
            [chunk] if final else [chunk, chunk],
            (place, field[0], own[0], flying[0], base_row, base_col[0], *back_x, *sy, order),
            [SMEM] + [VMEM] * 9 + [ANY],
            20,
        )
        cells = outs[0]
        if final:
            break
        field[0], send, keep[0], x_odd, extra = run(
            middle_kernel,
            f"middle_{sweep}",
            [chunk, half, half, pair, chunk],
            (strength, place, field[1], own[1], flying[1], cells, outs[1], rate_folded, first_folded, base_row, *base_col, *sx, *back_x, *sy),
            [SMEM] * 2 + [VMEM] * 16,
            32,
            [pltpu.VMEM(pair, f32)],
        )
        flying[0] = travel(send, 0)
        order = send
        second = later_second_kernel
    (result,) = run(
        last_kernel,
        "last",
        [(rows, cols)],
        (place, field[1], own[1], flying[1], cells, base_row, base_col[1], *back_x, *sy, mirx, miry),
        [SMEM] + [VMEM] * 12,
        24,
    )
    return result[None]


def solution(mesh):
    in_specs = (P("groups", None), P(("groups", "tm"), None, None), P(), P("groups"))
    out_specs = P(("groups", "tm"), None, None)
    return jax.shard_map(body, mesh=mesh, in_specs=in_specs, out_specs=out_specs, check_vma=False)
```

```python
import math

import jax
import jax.numpy as jnp
import numpy as np
from jax import lax
from jax.experimental import pallas as pl
from jax.experimental.pallas import tpu as pltpu
from jax.sharding import PartitionSpec as P

SWEEPS = 2
FIRST_LIMIT = 48

alpha_factor = 0.05
diffusion = 1.0
linear_part = 0.5
f32 = jnp.float32
bf16 = jnp.bfloat16
VMEM = pl.BlockSpec(memory_space=pltpu.VMEM)
SMEM = pl.BlockSpec(memory_space=pltpu.SMEM)
ANY = pl.BlockSpec(memory_space=pl.ANY)
HBM = pl.BlockSpec(memory_space=pltpu.HBM)


def halves(matrix):
    high = matrix.astype(bf16)
    low = (matrix - high.astype(np.float64)).astype(bf16)
    return high, low


def sine_half(order):
    ramp = np.arange(order // 2, dtype=np.int64) + 1
    folded = 2 * ramp[:, None] * ramp[None, :] % (2 * (order + 1))
    return math.sqrt(2.0 / (order + 1)) * np.sin(np.pi * folded / (order + 1))


def packed_tables(rows, cols):
    mirror = np.eye(math.gcd(rows // 2, cols // 2, 256))[::-1].astype(bf16)
    tables = (*halves(sine_half(rows)), *halves(sine_half(cols)), mirror)
    width = max(table.shape[0] for table in tables)
    shelves, spots = [], []
    row = col = height = 0
    for table in tables:
        size = table.shape[0]
        if not shelves or col + size > width or size > height:
            row, col, height = row + height, 0, size
            shelves.append(np.zeros((size, width), bf16))
        shelves[-1][:size, col : col + size] = table
        spots.append((row, col, size))
        col += size
    return jnp.asarray(np.concatenate(shelves)), tuple(spots)


def split(value):
    high = value.astype(bf16)
    return high, (value - high.astype(f32)).astype(bf16)


def product(left, right, dims=((1,), (0,))):
    return lax.dot_general(left, right, (dims, ((), ())), preferred_element_type=f32)


def apply_right(value, high, low):
    top, rest = split(value)
    return product(top, high) + (product(top, low) + product(rest, high))


def apply_left(high, low, value):
    top, rest = split(value)
    return product(high, top) + (product(low, top) + product(high, rest))


def forward(value, tx, ty):
    return apply_left(*tx, apply_right(value, *ty))


def backward(modes, tx, ty):
    return apply_right(apply_left(*tx, modes), *ty)


def signs(size, dim):
    shape = (size, 1) if dim == 0 else (1, size)
    return (1 - 2 * (lax.broadcasted_iota(jnp.int32, shape, dim) & 1)).astype(f32)


def eigenvalues(order, dim):
    half = order // 2
    shape = (order, 1) if dim == 0 else (1, order)
    slot = lax.broadcasted_iota(jnp.int32, shape, dim)
    number = jnp.where(slot < half, order - 1 - 2 * slot, 2 * (slot - half + 1))
    sines = jnp.sin(number.astype(f32) * (math.pi / (2.0 * (order + 1))))
    return 4.0 * sines * sines


def flip_rows(value, mirror):
    size = mirror.shape[0]
    count = value.shape[0] // size
    pieces = []
    for index in range(count):
        top, rest = split(value[(count - 1 - index) * size : (count - index) * size])
        pieces.append(product(mirror, top) + product(mirror, rest))
    return pieces[0] if count == 1 else jnp.concatenate(pieces, axis=0)


def flip_cols(value, mirror):
    size = mirror.shape[0]
    count = value.shape[1] // size
    pieces = []
    for index in range(count):
        top, rest = split(value[:, (count - 1 - index) * size : (count - index) * size])
        pieces.append(product(top, mirror) + product(rest, mirror))
    return pieces[0] if count == 1 else jnp.concatenate(pieces, axis=1)


def react(state, rate, strength):
    return strength * state * (linear_part - rate * (1.0 + state * state))


def gain(base_row, base_col, power=1):
    value = 1.0 / (base_row + base_col)
    while power > 1:
        value = value * value
        power //= 2
    return value


def bit_of(place, level):
    return lax.shift_right_logical(place[0], jnp.int32(level)) & 1


def kept_row(place, rows, level):
    row = jnp.int32(0)
    for index in range(level + 1):
        row = row + bit_of(place, index) * (rows >> (index + 1))
    return pl.multiple_of(row, math.gcd(rows >> (level + 1), 8))


def is_last(place, count):
    return place[0] == count - 1


def butterfly(quads, row):
    if row == 0:
        sign = signs(quads[0][0].shape[0], 0)
        left = sign * (quads[0][0] + quads[1][0])
        right = sign * (quads[0][1] + quads[1][1])
    else:
        left = quads[0][0] - quads[1][0]
        right = quads[0][1] - quads[1][1]
    return signs(left.shape[1], 1) * (left + right), left - right


def write_modes(place, modes, row, base_row, base_col, field, send, keep, less):
    hr = send.shape[0]
    block = pl.ds(pl.multiple_of(row * hr, 8), hr)
    value = modes * gain(base_row[block, :], base_col)
    field[block, :] = value
    upward = value if less is None else value - less
    bit = bit_of(place, 0)

    @pl.when(bit == row)
    def _():
        keep[...] = upward

    @pl.when(bit != row)
    def _():
        send[...] = upward


def take_modes(place, row, less, send, keep):
    @pl.when(bit_of(place, 0) == row)
    def _():
        keep[...] = keep[...] - less

    @pl.when(bit_of(place, 0) != row)
    def _():
        send[...] = send[...] - less


def first_kernel(count, spots, strength, place, u_hbm, rate_hbm, first_hbm, pack_hbm, field, send, keep, x_odd, xu_odd, base_row, base_col, txh, txl, tyh, tyl, mirror, u, rate, first, x_even, sems):
    rows, cols = u.shape
    hr, hc = rows // 2, cols // 2
    s = strength[0]
    targets = (u, rate, mirror, tyh, tyl, txh, txl)
    pieces = [pack_hbm.at[pl.ds(row, size), pl.ds(col, size)] for row, col, size in spots]
    sources = (u_hbm, rate_hbm, pieces[4], pieces[2], pieces[3], pieces[0], pieces[1])
    copies = [pltpu.make_async_copy(a, b, sems.at[i]) for i, (a, b) in enumerate(zip(sources, targets))]
    start = pltpu.make_async_copy(first_hbm, first, sems.at[len(copies)])
    for copy in copies:
        copy.start()

    @pl.when(place[0] == 0)
    def _():
        start.start()

    half_shift = 0.5 * (1.0 + linear_part * s)
    base_row[...] = half_shift + diffusion * eigenvalues(rows, 0)
    base_col[...] = half_shift + diffusion * eigenvalues(cols, 1)
    for copy in copies[:3]:
        copy.wait()

    def fold(value, even, odd):
        bottom = flip_rows(value[hr:], mirror[...])
        top = value[:hr]
        quads = (
            (top[:, :hc], flip_cols(top[:, hc:], mirror[...])),
            (bottom[:, :hc], flip_cols(bottom[:, hc:], mirror[...])),
        )
        for row in range(2):
            even[row], odd[row] = butterfly(quads, row)

    rate[...] = react(u[...], rate[...], s)

    @pl.when(place[0] == 0)
    def _():
        start.wait()
        rate[...] = rate[...] + first[...]

    fold(rate[...], x_even, x_odd)
    for copy in copies[3:]:
        copy.wait()

    tx, ty = (txh[...], txl[...]), (tyh[...], tyl[...])

    @pl.loop(0, 2)
    def _(row):
        modes = forward(x_even[row], tx, ty)
        write_modes(place, modes, row, base_row, base_col[:, :hc], field, send, keep, None)

    @pl.when(is_last(place, count))
    def _():
        fold(u[...], x_even, xu_odd)

        @pl.loop(0, 2)
        def _(row):
            take_modes(place, row, forward(x_even[row], tx, ty), send, keep)


def second_kernel(count, place, x_odd, xu_odd, txh, txl, tyh, tyl, base_row, base_col, order, field, send, keep):
    tx, ty = (txh[...], txl[...]), (tyh[...], tyl[...])
    hc = field.shape[1]

    @pl.loop(0, 2)
    def _(row):
        modes = forward(x_odd[row], tx, ty)
        write_modes(place, modes, row, base_row, base_col[:, hc:], field, send, keep, None)

    @pl.when(is_last(place, count))
    def _():
        @pl.loop(0, 2)
        def _(row):
            take_modes(place, row, forward(xu_odd[row], tx, ty), send, keep)


def later_second_kernel(count, place, x_odd, v_odd, txh, txl, tyh, tyl, base_row, base_col, order, field, send, keep):
    hr, hc = send.shape
    last = jnp.where(is_last(place, count), 1.0, 0.0)

    @pl.loop(0, 2)
    def _(row):
        modes = forward(x_odd[row], (txh[...], txl[...]), (tyh[...], tyl[...]))
        less = last * v_odd[pl.ds(pl.multiple_of(row * hr, 8), hr), :]
        write_modes(place, modes, row, base_row, base_col[:, hc:], field, send, keep, less)


def fold_kernel(place, rate, first, mirror, order, rate_out, first_out):
    hr, hc = rate.shape[0] // 2, rate.shape[1] // 2

    def fold(value, out):
        out[:hr, :hc] = value[:hr, :hc]
        out[:hr, hc:] = flip_cols(value[:hr, hc:], mirror[...])
        bottom = flip_rows(value[hr:], mirror[...])
        out[hr:, :hc] = bottom[:, :hc]
        out[hr:, hc:] = flip_cols(bottom[:, hc:], mirror[...])

    fold(rate, rate_out)

    @pl.when(place[0] == 0)
    def _():
        fold(first, first_out)

    @pl.when(place[0] != 0)
    def _():
        first_out[...] = jnp.zeros_like(first_out)


def rise_kernel(level, rows, col, place, keep, got, base_row, base_col, order, *outs):
    low = outs[0]
    half, width = keep.shape
    base_col = base_col[:, col * width : (col + 1) * width]
    bit = bit_of(place, level)
    row = kept_row(place, rows, level)
    own, other = keep[...], got[...]
    low[...] = jnp.where(bit == 0, own, other)
    factor = gain(base_row[pl.ds(row, half), :], base_col, 1 << level)
    total = jnp.where(bit == 0, other, own) + factor * low[...]
    if len(outs) == 2:
        outs[1][...] = total
        return
    quarter = half // 2
    send, keep_out = outs[1:]
    upper = bit_of(place, level + 1)
    send[...] = jnp.where(upper == 0, total[quarter:], total[:quarter])
    keep_out[...] = jnp.where(upper == 0, total[:quarter], total[quarter:])


def descend(place, level, rows, low, carry, base_row, base_col, own, send):
    half = low.shape[0]
    factor = gain(base_row[pl.ds(kept_row(place, rows, level), half), :], base_col, 1 << level)
    later = low[...] + factor * carry
    bit = bit_of(place, level)
    own[...] = jnp.where(bit == 0, carry, later)
    send[...] = jnp.where(bit == 0, later, carry)


def top_kernel(level, rows, col, place, mine, got, low, base_row, base_col, order, own, send):
    height, width = mine.shape
    base_col = base_col[:, col * width : (col + 1) * width]
    bit = bit_of(place, level)
    spot = pl.ds(kept_row(place, rows, level - 1), height)
    value = 1.0 / (base_row[spot, :] + base_col)
    factor = value
    for _ in range(level):
        factor = factor * factor
    early = jnp.where(bit == 0, mine[...], got[...])
    late = jnp.where(bit == 0, got[...], mine[...])
    carry = alpha_factor * (late + factor * early) / (1.0 - alpha_factor * (factor * factor))
    carry = jnp.where(bit == 0, carry, early + factor * carry)
    descend(place, level - 1, rows, low, carry, base_row, base_col, own, send)


def fall_kernel(level, rows, col, place, own_in, got, low, base_row, base_col, order, own, send):
    width = own_in.shape[1]
    base_col = base_col[:, col * width : (col + 1) * width]
    bit = bit_of(place, level + 1)
    first = jnp.where(bit == 0, own_in[...], got[...])
    second = jnp.where(bit == 0, got[...], own_in[...])
    carry = jnp.concatenate([first, second], axis=0)
    descend(place, level, rows, low, carry, base_row, base_col, own, send)


def new_modes(place, row, field, own, got, base_row, base_col):
    hr = own.shape[0]
    block = pl.ds(pl.multiple_of(row * hr, 8), hr)
    carry = jnp.where(bit_of(place, 0) == row, own[...], got[...])
    return field[block, :] + gain(base_row[block, :], base_col) * carry


def half_back_kernel(place, field, own, got, base_row, base_col, txh, txl, tyh, tyl, order, cells, *v_out):
    hr, hc = own.shape
    tx, ty = (txh[...], txl[...]), (tyh[...], tyl[...])
    parts = []
    for row in range(2):
        modes = new_modes(place, row, field, own, got, base_row, base_col[:, :hc])
        if v_out:
            v_out[0][row * hr : (row + 1) * hr, :] = modes
        parts.append(backward(modes, tx, ty) * signs(hc, 1))
    parts[0] = parts[0] * signs(hr, 0)
    cells[:hr, :] = parts[0] + parts[1]
    cells[hr:, :] = parts[0] - parts[1]


def odd_cells(place, field, own, got, base_row, base_col, tx, ty, v_out):
    hr, hc = own.shape
    parts = []
    for row in range(2):
        modes = new_modes(place, row, field, own, got, base_row, base_col[:, hc:])
        if v_out is not None:
            v_out[row * hr : (row + 1) * hr, :] = modes
        parts.append(backward(modes, tx, ty))
    parts[0] = parts[0] * signs(hr, 0)
    return parts[0] + parts[1], parts[0] - parts[1]


def middle_kernel(count, strength, place, field_in, own, got, cells, v_even, rate, first, base_row, base_col, txh, txl, tyh, tyl, field, send, keep, x_odd, v_odd, x_even):
    hr, hc = own.shape
    s = strength[0]
    tx, ty = (txh[...], txl[...]), (tyh[...], tyl[...])
    odd = odd_cells(place, field_in, own, got, base_row, base_col, tx, ty, v_odd)
    quads = []
    for half in range(2):
        rows = slice(half * hr, (half + 1) * hr)
        even = cells[rows, :]
        quads.append(
            (
                react(even + odd[half], rate[rows, :hc], s) + first[rows, :hc],
                react(even - odd[half], rate[rows, hc:], s) + first[rows, hc:],
            )
        )
    for row in range(2):
        x_even[row], x_odd[row] = butterfly(quads, row)
    last = jnp.where(is_last(place, count), 1.0, 0.0)

    @pl.loop(0, 2)
    def _(row):
        modes = forward(x_even[row], tx, ty)
        less = last * v_even[pl.ds(pl.multiple_of(row * hr, 8), hr), :]
        write_modes(place, modes, row, base_row, base_col[:, :hc], field, send, keep, less)


def last_kernel(place, field_in, own, got, cells, base_row, base_col, txh, txl, tyh, tyl, mirror, out):
    hr, hc = own.shape
    odd = odd_cells(place, field_in, own, got, base_row, base_col, (txh[...], txl[...]), (tyh[...], tyl[...]), None)
    out[:hr, :hc] = cells[:hr, :] + odd[0]
    out[:hr, hc:] = flip_cols(cells[:hr, :] - odd[0], mirror[...])
    bottom = flip_rows(jnp.concatenate([cells[hr:, :] + odd[1], cells[hr:, :] - odd[1]], axis=1), mirror[...])
    out[hr:, :hc] = bottom[:, :hc]
    out[hr:, hc:] = flip_cols(bottom[:, hc:], mirror[...])


def run(kernel, name, outs, operands, specs, limit, scratch=()):
    return pl.pallas_call(
        kernel,
        out_shape=[out if hasattr(out, "dtype") else jax.ShapeDtypeStruct(out, f32) for out in outs],
        in_specs=specs,
        out_specs=[VMEM] * len(outs),
        scratch_shapes=list(scratch),
        compiler_params=pltpu.CompilerParams(vmem_limit_bytes=limit << 20),
        cost_estimate=pl.CostEstimate(flops=0, bytes_accessed=1024, transcendentals=0),
        name=name,
    )(*operands)


def body(initial_value, guess, rate_field, strength):
    count = lax.axis_size("tm")
    levels = count.bit_length() - 1
    place = lax.axis_index("tm").reshape(1)
    state = guess[0]
    rows, cols = state.shape
    hr, hc = rows // 2, cols // 2

    pack, spots = packed_tables(rows, cols)

    def travel(value, level):
        return lax.ppermute(value, "tm", [(source, source ^ (1 << level)) for source in range(count)])

    def bind(kernel, *static):
        return lambda *refs: kernel(*static, *refs)

    chunk, half = (rows, hc), (hr, hc)
    pair = (2, hr, hc)
    field = [None, None]
    keep = [None, None]
    flying = [None, None]

    field[0], send, keep[0], x_odd, extra, *others = run(
        bind(first_kernel, count, spots),
        "first",
        [chunk, half, half, pair, pair, (rows, 1), (1, cols)]
        + [jax.ShapeDtypeStruct((size, size), bf16) for _, _, size in spots],
        (strength, place, state, rate_field, initial_value, pack),
        [SMEM] * 2 + [HBM] * 4,
        FIRST_LIMIT,
        [pltpu.VMEM((rows, cols), f32)] * 3 + [pltpu.VMEM(pair, f32), pltpu.SemaphoreType.DMA((8,))],
    )
    bases, tables, mirror = others[:2], others[2:6], others[6]
    flying[0] = travel(send, 0)
    order = send
    second = second_kernel
    rate_folded = first_folded = None

    for sweep in range(SWEEPS):
        final = sweep == SWEEPS - 1
        field[1], send, keep[1] = run(
            bind(second, count),
            f"second_{sweep}",
            [chunk, half, half],
            (place, x_odd, extra, *tables, *bases, order),
            [SMEM] + [VMEM] * 8 + [ANY],
            16,
        )
        flying[1] = travel(send, 0)
        order = send
        low = [[], []]
        own = [None, None]
        for level in range(levels - 1):
            for col in range(2):
                height = rows >> (level + 1)
                full = level == levels - 2
                shapes = [(height, hc)] + ([(height, hc)] if full else [(height // 2, hc)] * 2)
                outs = run(
                    bind(rise_kernel, level, rows, col),
                    f"rise_{sweep}_{level}_{col}",
                    shapes,
                    (place, keep[col], flying[col], *bases, order),
                    [SMEM] + [VMEM] * 4 + [ANY],
                    8,
                )
                low[col].append(outs[0])
                keep[col] = outs[-1]
                order = outs[1]
                flying[col] = travel(outs[1], level + 1)
            if sweep == 0 and level == 0:
                rate_folded, first_folded = run(
                    fold_kernel,
                    "fold",
                    [(rows, cols)] * 2,
                    (place, rate_field, initial_value, mirror, order),
                    [SMEM] + [VMEM] * 3 + [ANY],
                    20,
                )
                order = rate_folded
        for level in range(levels - 2, -1, -1):
            for col in range(2):
                height = rows >> (level + 1)
                top = level == levels - 2
                own[col], send = run(
                    bind(top_kernel, levels - 1, rows, col) if top else bind(fall_kernel, level, rows, col),
                    f"fall_{sweep}_{level}_{col}",
                    [(height, hc)] * 2,
                    (place, keep[col] if top else own[col], flying[col], low[col][level], *bases, order),
                    [SMEM] + [VMEM] * 5 + [ANY],
                    8,
                )
                order = send
                flying[col] = travel(send, level)
        outs = run(
            half_back_kernel,
            f"back_{sweep}",
            [chunk] if final else [chunk, chunk],
            (place, field[0], own[0], flying[0], *bases, *tables, order),
            [SMEM] + [VMEM] * 9 + [ANY],
            16,
        )
        cells = outs[0]
        if final:
            break
        field[0], send, keep[0], x_odd, extra = run(
            bind(middle_kernel, count),
            f"middle_{sweep}",
            [chunk, half, half, pair, chunk],
            (strength, place, field[1], own[1], flying[1], cells, outs[1], rate_folded, first_folded, *bases, *tables),
            [SMEM] * 2 + [VMEM] * 13,
            28,
            [pltpu.VMEM(pair, f32)],
        )
        flying[0] = travel(send, 0)
        order = send
        second = later_second_kernel
    (result,) = run(
        last_kernel,
        "last",
        [(rows, cols)],
        (place, field[1], own[1], flying[1], cells, *bases, *tables, mirror),
        [SMEM] + [VMEM] * 11,
        20,
    )
    return result[None]


def solution(mesh):
    in_specs = (P("groups", None), P(("groups", "tm"), None, None), P(), P("groups"))
    out_specs = P(("groups", "tm"), None, None)
    return jax.shard_map(body, mesh=mesh, in_specs=in_specs, out_specs=out_specs, check_vma=False)
```
